32 devices in a mesh: delay: 8 (over z, y), rows: 4 (over x, core).
Axes of the slice: x: 2, y: 2, z: 4, core: 2. Of those that a mesh axis runs over, the one named last changes fastest.
Arguments:
- retarded: bfloat16 [8, 24, 12, 128, 128], P('delay', 'rows'), may hold values from -0.078125 to 0.078125
- sources: int32 [8, 24, 12], P('delay', 'rows'), may hold values from 0 to 23, as said below
- self_inverse: float32 [24, 128, 128], P('rows'), may hold values from -2 to 2, as said below
- excitation: bfloat16 [2, 3072, 128], P(None, 'rows'), may hold values from -6 to 6
- pending: float32 [8, 3072, 128], P('delay', 'rows'), may hold values from -6 to 6
Outputs:
- densities: bfloat16 [2, 3072, 128], P(None, 'rows')
- sums_after: float32 [8, 3072, 128], P('delay', 'rows')
The draws below stay inside these ranges and needn't reach their ends.
Inputs may be any that keep to these rules, and one draw needn't show every extreme that they name: `sources`: each row block of each delay lists 12 different source blocks. `self_inverse`: each block is a diagonal of 0.5 to 1.5 plus small full coupling.
All inputs are finite; a program needn't handle non-finite values.
Results may differ from the reference program's by a relative error of at most 0.0034.
Values may be sent and summed in bfloat16 or wider, within the bound.
No kernel may reach another device: no remote copies, remote signals or barrier semaphores. Data moves between devices by JAX's collectives and lax.ppermute only.
A program may use at most 64 MiB of HBM per device.

```python
import math
import jax
import jax.numpy as jnp
from jax import lax

PATCH = 3072
BLK = 128
NBLK = 24
LIST = 12
EXC = 128
DELAYS = 8
STEPS = 2


def draw_sources(key, part):
    subkeys = jax.random.split(key, DELAYS * NBLK)
    chosen = jax.vmap(lambda single: jax.random.permutation(single, NBLK)[:LIST])(subkeys)
    return chosen.reshape(DELAYS, NBLK, LIST).astype(jnp.int32)


def draw_self_inverse(key, part):
    first_key, second_key = jax.random.split(key)
    coupling = jnp.clip(jax.random.normal(first_key, (NBLK, BLK, BLK), jnp.float32), -4.0, 4.0) * (0.6 / math.sqrt(BLK))
    diagonal = jax.random.uniform(second_key, (NBLK, BLK), jnp.float32, 0.5, 1.5)
    return coupling + diagonal[:, :, None] * jnp.eye(BLK, dtype=jnp.float32)


def levels(stream_key, extent, shards, smallest, largest):
    def one(axis_at, blocks):
        steps = jax.random.uniform(jax.random.fold_in(jax.random.fold_in(stream_key, 6), axis_at), (blocks,), jnp.float32, smallest / len(shards), largest / len(shards))
        return jnp.repeat(jnp.exp(steps), extent[axis_at] // blocks).reshape((-1,) + (1,) * (len(extent) - axis_at - 1))

    factor_of = one(*shards[0])
    for cut in shards[1:]:
        factor_of = factor_of * one(*cut)
    return factor_of


def normal_values(own_key, shape, deviation, reach, shards=(), held_as=jnp.bfloat16):
    entries = jax.random.normal(own_key, shape, jnp.float32) * deviation
    if len(shards) > 0:
        entries = levels(own_key, shape, shards, -0.22, 0.18) * entries
    return jnp.clip(entries, min=-reach, max=reach).astype(held_as)


def setup_inputs(seed: int = 0) -> dict:
    streams_of = jax.random.split(jax.random.key(seed), 6)
    retarded = normal_values(streams_of[0], (DELAYS, NBLK, LIST, BLK, BLK), (4 * LIST * BLK) ** -0.5, 0.078125, ((0, 8), (1, 4)))
    sources = draw_sources(jax.random.fold_in(streams_of[5], 71), 0)
    self_inverse = draw_self_inverse(jax.random.fold_in(streams_of[5], 71), 0)
    excitation = normal_values(streams_of[3], (STEPS, PATCH, EXC), 1.0, 6.0, ((1, 4),))
    pending = normal_values(streams_of[4], (DELAYS, PATCH, EXC), 1.0, 6.0, ((0, 8), (1, 4)), jnp.float32)
    return dict(retarded=retarded, sources=sources, self_inverse=self_inverse, excitation=excitation, pending=pending)


def reference(retarded, sources, self_inverse, excitation, pending):
    pending_sums = pending
    collected = []
    for step_index in range(STEPS):
        right_side = excitation[step_index].astype(jnp.float32) - pending_sums[0]
        solved = jnp.einsum("bij,bjc->bic", self_inverse, right_side.reshape(NBLK, BLK, EXC), precision=lax.Precision.HIGHEST)
        density = solved.astype(jnp.bfloat16).reshape(PATCH, EXC)
        collected.append(density)
        blocks = density.reshape(NBLK, BLK, EXC)

        def one_delay(pair):
            delay_blocks, delay_sources = pair
            picked = jnp.take(blocks, delay_sources.reshape(-1), axis=0).reshape(NBLK, LIST, BLK, EXC)
            terms = jnp.einsum("rlij,rljc->ric", delay_blocks.astype(jnp.float32), picked.astype(jnp.float32))
            return terms.reshape(PATCH, EXC)

        terms_all = lax.map(one_delay, (retarded, sources))
        shifted = jnp.concatenate([pending_sums[1:], jnp.zeros((1, PATCH, EXC), jnp.float32)], axis=0)
        pending_sums = shifted + terms_all
    return jnp.stack(collected), pending_sums
```

```python
import functools

import jax
import jax.numpy as jnp
from jax import lax
from jax.experimental import pallas as pl
from jax.experimental.pallas import tpu as pltpu
from jax.sharding import PartitionSpec as P

BOTH = ("delay", "rows")
VMEM_BYTES = 12 << 20


def call(kernel, out_shape, operands, scratch=(), flops=0, aliases=None):
    specs = [
        pl.BlockSpec(memory_space=pltpu.SMEM if a.dtype == jnp.int32 else pltpu.VMEM)
        for a in operands
    ]
    many = isinstance(out_shape, (tuple, list))
    vmem = pl.BlockSpec(memory_space=pltpu.VMEM)
    moved = sum(a.size * a.dtype.itemsize for a in operands)
    return pl.pallas_call(
        kernel,
        out_shape=out_shape,
        in_specs=specs,
        out_specs=[vmem] * len(out_shape) if many else vmem,
        scratch_shapes=list(scratch),
        input_output_aliases=aliases or {},
        compiler_params=pltpu.CompilerParams(vmem_limit_bytes=VMEM_BYTES),
        cost_estimate=pl.CostEstimate(
            flops=flops, bytes_accessed=moved, transcendentals=0
        ),
    )(*operands)


def solve(inverse, right):
    product = jnp.dot(
        inverse,
        right,
        precision=lax.Precision.HIGHEST,
        preferred_element_type=jnp.float32,
    )
    return product.astype(jnp.bfloat16)


def assemble(pieces, parts, table):
    own = lax.axis_index("rows")
    part = lax.rem(lax.axis_index("delay"), parts)
    per = pieces[0].shape[0]
    for i, piece in enumerate(pieces):
        owner = own ^ (i // parts)
        at = (owner * parts + (part ^ (i % parts))) * per
        table[pl.ds(at, per)] = piece[...]


def listed(retarded, sources, table, row):
    count = retarded.shape[2]
    total = None
    for first in range(0, count, 2):
        entries = range(first, min(first + 2, count))
        left = jnp.concatenate([retarded[0, row, e] for e in entries], axis=1)
        right = jnp.concatenate([table[sources[0, row, e]] for e in entries], axis=0)
        term = jnp.dot(left, right, preferred_element_type=jnp.float32)
        total = term if total is None else total + term
    return total


def first_density(inverse, excitation, pending, out):
    for b in range(inverse.shape[0]):
        right = excitation[b].astype(jnp.float32) - pending[b]
        out[b] = solve(inverse[b], right)


def next_density(parts, count, sources, retarded, inverse, excitation, due, *rest):
    pieces, out, table = rest[:count], rest[count], rest[count + 1]
    assemble(pieces, parts, table)
    for b in range(inverse.shape[0]):
        accum = due[b] + listed(retarded, sources, table, b)
        right = excitation[b].astype(jnp.float32) - accum
        out[b] = solve(inverse[b], right)


def add_terms(parts, count, sources, retarded, due, *rest):
    pieces, (total, own, table) = rest[:count], rest[count:]
    assemble(pieces, parts, table)
    blocks = total.shape[0]
    for b in range(blocks):
        total[b] = due[b] + listed(retarded, sources, table, b)
    own[...] = table[pl.ds(lax.axis_index("rows") * blocks, blocks)]


def permuted(block, pairs):
    return lax.ppermute(block, BOTH, pairs)


def on_device(retarded, sources, self_inverse, excitation, pending):
    delays, owners = lax.axis_size("delay"), lax.axis_size("rows")
    blocks, count, size = retarded.shape[1:4]
    columns = excitation.shape[2]
    shape = (blocks, size, columns)
    parts = 2 if delays % 2 == 0 and blocks % 2 == 0 else 1
    high = delays // parts
    place = lax.axis_index("delay")
    low_at, high_at = lax.rem(place, parts), place // parts
    excited = excitation.reshape(2, *shape)
    terms = 2 * blocks * count * size * size * columns
    table = pltpu.VMEM((owners * blocks, size, columns), jnp.bfloat16)
    density = jax.ShapeDtypeStruct(shape, jnp.bfloat16)
    sums = jax.ShapeDtypeStruct(shape, jnp.float32)

    def at(d, r):
        return d * owners + r

    def everywhere(move):
        return [
            (at(d, r), at(*move(d, r))) for d in range(delays) for r in range(owners)
        ]

    def shift(block):
        return permuted(
            block,
            [(at(d, r), at(d - 1, r)) for d in range(1, delays) for r in range(owners)],
        )

    def over_rows(pieces):
        bit = owners // 2
        found = {0: pieces}
        while bit:
            got = {
                key ^ bit: [
                    permuted(p, everywhere(lambda d, r: (d, r ^ bit))) for p in value
                ]
                for key, value in found.items()
            }
            found.update(got)
            bit //= 2
        return [p for key in range(owners) for p in found[key]]

    def spread(block):
        per = blocks // parts
        piece = block[:per]
        if parts == 2:
            sent = permuted(block[per:], [(at(0, r), at(1, r)) for r in range(owners)])
            piece = jnp.where(low_at == 0, piece, sent)
        step = high
        while step > 1:
            step //= 2
            pairs = [
                (at(h * parts + y, r), at((h + step) * parts + y, r))
                for h in range(0, high - step, 2 * step)
                for y in range(parts)
                for r in range(owners)
            ]
            got = permuted(piece, pairs)
            piece = jnp.where(lax.rem(high_at, 2 * step) == step, got, piece)
        return piece

    def in_plane(piece):
        pieces = [piece]
        if parts == 2:
            pieces.append(permuted(piece, everywhere(lambda d, r: (d ^ 1, r))))
        return over_rows(pieces)

    due_first = shift(pending)[0].reshape(shape)
    density_0 = call(
        first_density, density, (self_inverse, excited[0], pending.reshape(shape))
    )
    near = over_rows([density_0])
    density_1 = call(
        functools.partial(next_density, 1, len(near)),
        density,
        (sources, retarded, self_inverse, excited[1], due_first, *near),
        [table],
        terms,
    )
    pieces = in_plane(spread(density_0))
    accum, own_0 = call(
        functools.partial(add_terms, parts, len(pieces)),
        (sums, density),
        (sources, retarded, due_first, *pieces),
        [table],
        terms,
    )
    due_second = shift(accum)
    pieces = in_plane(spread(density_1))
    total, own_1 = call(
        functools.partial(add_terms, parts, len(pieces)),
        (sums, density),
        (sources, retarded, due_second, *pieces),
        [table],
        terms,
    )
    collected = jnp.stack([own_0, own_1]).reshape(excitation.shape)
    return collected, total.reshape(pending.shape)


def solution(mesh):
    placed = (
        P("delay", "rows", None, None, None),
        P("delay", "rows", None),
        P("rows", None, None),
        P(None, "rows", None),
        P("delay", "rows", None),
    )
    return jax.shard_map(
        on_device,
        mesh=mesh,
        in_specs=placed,
        out_specs=(P(None, "rows", None), P("delay", "rows", None)),
        check_vma=False,
    )
```
